32 devices in a mesh: sa: 8 (over y, x, core), tp: 4 (over z).
Axes of the slice: x: 2, y: 2, z: 4, core: 2. Of those that a mesh axis runs over, the one named last changes fastest.
Arguments:
- window: float32 [2, 2, 16, 32, 512], P(None, None, 'sa', None, 'tp'), may hold values from -4 to 4
- damping: float32 [16, 32], P('sa'), may hold values from 0 to 1
- propagator: float32 [2, 32, 32], replicated, may hold values from -1 to 1, as said below
- coupling: float32 [32], replicated, may hold values from 0.5 to 1.5
Outputs:
- lesser_next: float32 [2, 16, 32, 512], P(None, 'sa', None, 'tp')
The draws below stay inside these ranges and needn't reach their ends.
Inputs may be any that keep to these rules, and one draw needn't show every extreme that they name: `propagator`: a unitary matrix.
All inputs are finite; a program needn't handle non-finite values.
Results may differ from the reference program's by a relative error of at most 0.0079.
Values may be sent and summed in bfloat16 or wider, within the bound.
A program may use at most 64 MiB of HBM per device.

```python
import math
import jax
import jax.numpy as jnp
from jax import lax

NO = 32
T_SIZE = 16


def draw_propagator(key, part):
    key_real = jax.random.fold_in(key, 11)
    key_imag = jax.random.fold_in(key, 12)
    sample_re = jax.random.normal(key_real, (NO, NO), jnp.float32)
    sample_im = jax.random.normal(key_imag, (NO, NO), jnp.float32)
    hermitian = ((sample_re + sample_re.T) * 0.5 + 1j * (sample_im - sample_im.T) * 0.5) * (1.5 / jnp.sqrt(NO * 1.0))
    identity = jnp.eye(NO, dtype=jnp.complex64)
    unitary = jnp.linalg.solve(identity + 0.5j * hermitian, identity - 0.5j * hermitian)
    return jnp.stack([jnp.real(unitary), jnp.imag(unitary)]).astype(jnp.float32)


def draw_damping(key, part):
    key_fast = jax.random.fold_in(key, 21)
    key_slow = jax.random.fold_in(key, 22)
    key_quick = jax.random.fold_in(key, 23)
    key_modulate = jax.random.fold_in(key, 24)
    key_spots = jax.random.fold_in(key, 25)
    key_factors = jax.random.fold_in(key, 26)
    fast_share = 0.5
    fast = jax.random.uniform(key_fast, (NO,), jnp.float32) < fast_share
    slow_rate = jax.random.uniform(key_slow, (NO,), jnp.float32, 0.05, 0.8) / T_SIZE
    quick_rate = jax.random.uniform(key_quick, (NO,), jnp.float32, 1.0 / 50.0, 1.0 / 30.0)
    relaxation_speeds = jnp.where(fast, quick_rate, slow_rate)
    forcing_envelope = jnp.exp(jax.random.uniform(key_modulate, (T_SIZE, 1), jnp.float32, -0.7, 0.7))
    excitation_locations = jax.random.randint(key_spots, (3,), 0, T_SIZE)
    amplitude_multipliers = jax.random.uniform(key_factors, (3,), jnp.float32, 0.6, 0.85)
    lattice_coordinates = jnp.arange(T_SIZE)[:, None]
    excitation_episodes = jnp.prod(jnp.where(lattice_coordinates == excitation_locations[None, :], amplitude_multipliers[None, :], 1.0), axis=1)
    return (jnp.exp(-relaxation_speeds[None, :] * forcing_envelope) * excitation_episodes[:, None]).astype(jnp.float32)


def block_scale(rng, extent, cuts, low, high):
    gain, own = 1.0, jax.random.fold_in(rng, 6)
    for dim, parts in cuts:
        steps = jnp.exp(jax.random.uniform(jax.random.fold_in(own, dim), (parts,), jnp.float32, low / len(cuts), high / len(cuts)))
        gain = gain * jnp.repeat(steps, extent[dim] // parts).reshape([-1 if axis == dim else 1 for axis in range(len(extent))])
    return gain


def centred(rng, shape, scale, reach, split=(), kind=jnp.bfloat16):
    drawn = jax.random.normal(rng, shape, jnp.float32) * scale
    if len(split) > 0:
        drawn = block_scale(rng, shape, split, -0.22, 0.18) * drawn
    return jnp.clip(drawn, min=-reach, max=reach).astype(kind)


def setup_inputs(seed: int = 0) -> dict:
    seeds = jax.random.split(jax.random.key(seed), 5)
    window = centred(seeds[0], (2, 2, T_SIZE, NO, T_SIZE * NO), 1.0, 4.0, ((2, 8), (4, 4)), jnp.float32)
    damping = draw_damping(jax.random.fold_in(seeds[4], 71), 0)
    propagator = draw_propagator(jax.random.fold_in(seeds[4], 71), 0)
    coupling = jnp.clip(jnp.exp(jax.random.uniform(seeds[3], (NO,), jnp.float32, math.log(0.5), math.log(1.5))), 0.5, 1.5)
    return dict(window=window, damping=damping, propagator=propagator, coupling=coupling)


highest = lax.Precision.HIGHEST

def spectral_self_energy(occupied_correlator, greater, coupling, column_tiles):
    factor = jnp.tile(coupling[:, None] * coupling[None, :], (1, column_tiles))
    less_re, less_im = (occupied_correlator[0], occupied_correlator[1])
    great_re, great_im = (greater[0], greater[1])
    lsquare_re = less_re * less_re - less_im * less_im
    lsquare_im = 2.0 * less_re * less_im
    gsquare_re = great_re * great_re - great_im * great_im
    gsquare_im = 2.0 * great_re * great_im
    sless_re = -factor * (lsquare_re * great_re + lsquare_im * great_im)
    sless_im = -factor * (lsquare_im * great_re - lsquare_re * great_im)
    sgreat_re = -factor * (gsquare_re * less_re + gsquare_im * less_im)
    sgreat_im = -factor * (gsquare_im * less_re - gsquare_re * less_im)
    return jnp.stack([sgreat_re - sless_re, sgreat_im - sless_im]).astype(jnp.bfloat16)

def complex_product(left_re, left_im, right_re, right_im):
    cosine_component = jnp.dot(left_re, right_re, precision=highest) - jnp.dot(left_im, right_im, precision=highest)
    imag_part = jnp.dot(left_re, right_im, precision=highest) + jnp.dot(left_im, right_re, precision=highest)
    return (cosine_component, imag_part)

def collision_term(spectral, history, weight_scale):
    width = spectral.shape[1] * spectral.shape[2]
    left_re = spectral[0].reshape(width, width)
    left_im = spectral[1].reshape(width, width)
    right_re = history[0].reshape(width, width)
    right_im = history[1].reshape(width, width)
    cosine_component = jnp.dot(left_re.astype(jnp.float32), right_re.astype(jnp.float32), preferred_element_type=jnp.float32) - jnp.dot(left_im.astype(jnp.float32), right_im.astype(jnp.float32), preferred_element_type=jnp.float32)
    imag_part = jnp.dot(left_re.astype(jnp.float32), right_im.astype(jnp.float32), preferred_element_type=jnp.float32) + jnp.dot(left_im.astype(jnp.float32), right_re.astype(jnp.float32), preferred_element_type=jnp.float32)
    return weight_scale * jnp.stack([cosine_component, imag_part]).reshape(history.shape)

def propagate(forcing, damping, propagator, initial):

    def advance(state, inputs):
        damp_row, force_row = inputs
        cosine_component, imag_part = complex_product(propagator[0], propagator[1], state[0], state[1])
        advanced = damp_row[None, :, None] * jnp.stack([cosine_component, imag_part]) + force_row
        return (advanced, advanced)
    last_state, produced = lax.scan(advance, initial, (damping, jnp.moveaxis(forcing, 1, 0)))
    return jnp.moveaxis(produced, 0, 1)

def reference(window, damping, propagator, coupling):
    occupied_correlator = window[0]
    greater = window[1]
    initial = occupied_correlator[:, 0]
    weight_scale = 1.0 / (T_SIZE * math.sqrt(NO))
    first_spectral = spectral_self_energy(occupied_correlator, greater, coupling, T_SIZE)
    first_term = collision_term(first_spectral, occupied_correlator.astype(jnp.bfloat16), weight_scale)
    predicted = propagate(first_term, damping, propagator, initial)
    second_spectral = spectral_self_energy(predicted, greater, coupling, T_SIZE)
    second_term = collision_term(second_spectral, predicted.astype(jnp.bfloat16), weight_scale)
    return propagate(0.5 * (first_term + second_term), damping, propagator, initial)
```

```python
import functools
import math

import jax
import jax.numpy as jnp
from jax import lax
from jax.experimental import pallas as pl
from jax.experimental.pallas import tpu as pltpu
from jax.sharding import PartitionSpec as P

MESH = pl.DeviceIdType.MESH
F32 = jnp.float32
BF16 = jnp.bfloat16


def exact(a, b):
    return jnp.dot(a, b, precision=lax.Precision.HIGHEST, preferred_element_type=F32)


def split(x):
    high = x.astype(BF16)
    return high, (x - high.astype(F32)).astype(BF16)


def mm(a, b):
    return jnp.dot(a, b, preferred_element_type=F32)


def mm3(a, b):
    return mm(a[0], b[0]) + (mm(a[0], b[1]) + mm(a[1], b[0]))


def spectral_of(x_re, x_im, g_re, g_im, factor):
    lsquare_re = x_re * x_re - x_im * x_im
    lsquare_im = 2.0 * x_re * x_im
    gsquare_re = g_re * g_re - g_im * g_im
    gsquare_im = 2.0 * g_re * g_im
    sless_re = -factor * (lsquare_re * g_re + lsquare_im * g_im)
    sless_im = -factor * (lsquare_im * g_re - lsquare_re * g_im)
    sgreat_re = -factor * (gsquare_re * x_re + gsquare_im * x_im)
    sgreat_im = -factor * (gsquare_im * x_re - gsquare_re * x_im)
    return jnp.concatenate([sgreat_re - sless_re, sgreat_im - sless_im], axis=0).astype(BF16)


def kernel(
    n_sa, n_tp, scale,
    win, damp, prop, coup, out,
    dall, hist, spec1, off, fev, hist2, spec2, off2, w_hi, w_lo,
    s_d, r_d, s_h, r_h, s_s1, r_s1, s_o, r_o, s_f, r_f, s_s2, r_s2, s_o2, r_o2,
):
    me_sa = lax.axis_index("sa")
    me_tp = lax.axis_index("tp")
    no = prop.shape[1]
    cols = win.shape[4]
    rows = win.shape[2] * no

    barrier = pltpu.get_barrier_semaphore()
    for k in range(1, n_sa):
        pl.semaphore_signal(
            barrier, inc=1, device_id=(lax.rem(me_sa + k, n_sa), me_tp), device_id_type=MESH
        )
    for k in range(1, n_tp):
        pl.semaphore_signal(
            barrier, inc=1, device_id=(me_sa, lax.rem(me_tp + k, n_tp)), device_id_type=MESH
        )

    def sa_copy(buf, send, recv, k):
        return pltpu.make_async_remote_copy(
            src_ref=buf.at[me_sa], dst_ref=buf.at[me_sa], send_sem=send.at[k - 1],
            recv_sem=recv.at[me_sa],
            device_id=(lax.rem(me_sa + k, n_sa), me_tp), device_id_type=MESH,
        )

    def sa_wait(buf, send, recv, k):
        who = lax.rem(me_sa + k, n_sa)
        pltpu.make_async_remote_copy(
            src_ref=buf.at[who], dst_ref=buf.at[who], send_sem=send.at[k - 1],
            recv_sem=recv.at[who], device_id=(who, me_tp), device_id_type=MESH,
        ).wait_recv()

    def tp_copy(buf, send, recv, k):
        return pltpu.make_async_remote_copy(
            src_ref=buf.at[me_tp], dst_ref=buf.at[me_tp], send_sem=send.at[k - 1],
            recv_sem=recv.at[me_tp],
            device_id=(me_sa, lax.rem(me_tp + k, n_tp)), device_id_type=MESH,
        )

    def tp_wait(buf, send, recv, k):
        who = lax.rem(me_tp + k, n_tp)
        pltpu.make_async_remote_copy(
            src_ref=buf.at[who], dst_ref=buf.at[who], send_sem=send.at[k - 1],
            recv_sem=recv.at[who], device_id=(me_sa, who), device_id_type=MESH,
        ).wait_recv()

    pending = []

    def send_sa(buf, send, recv):
        for k in range(1, n_sa):
            copy = sa_copy(buf, send, recv, k)
            copy.start()
            pending.append(copy)

    def send_tp(buf, send, recv):
        for k in range(1, n_tp):
            copy = tp_copy(buf, send, recv, k)
            copy.start()
            pending.append(copy)

    row_id = lax.broadcasted_iota(jnp.int32, (no, cols), 0)
    lane_id = lax.broadcasted_iota(jnp.int32, (no, cols), 1)
    tiled = (lax.rem(lane_id, no) == row_id).astype(F32)
    c_row = coup[...]
    c_lanes = exact(c_row, tiled)
    eye = lax.broadcasted_iota(jnp.int32, (no, no), 0) == lax.broadcasted_iota(jnp.int32, (no, no), 1)
    c_col = jnp.sum(jnp.where(eye, jnp.broadcast_to(c_row, (no, no)), 0.0), axis=1, keepdims=True)
    factor = c_col * c_lanes
    factor = jnp.concatenate([factor] * win.shape[2], axis=0)

    l_re = win[0, 0].reshape(rows, cols)
    l_im = win[0, 1].reshape(rows, cols)
    g_re = win[1, 0].reshape(rows, cols)
    g_im = win[1, 1].reshape(rows, cols)
    dmine = dall.at[me_sa]
    dmine[...] = jnp.zeros(dmine.shape, F32)
    dmine[0:2, 0:no] = damp[...]
    hmine = hist.at[me_sa]
    hmine[:, 0:cols] = l_re.astype(BF16)
    hmine[:, cols : 2 * cols] = l_im.astype(BF16)
    spec1[me_tp] = spectral_of(l_re, l_im, g_re, g_im, factor)

    pl.semaphore_wait(barrier, n_sa + n_tp - 2)
    send_tp(spec1, s_s1, r_s1)
    send_sa(dall, s_d, r_d)
    send_sa(hist, s_h, r_h)

    first = (lax.broadcasted_iota(jnp.int32, (no, 2 * no), 0)
             == lax.broadcasted_iota(jnp.int32, (no, 2 * no), 1)).astype(F32)
    second = (lax.broadcasted_iota(jnp.int32, (no, 2 * no), 0) + no
              == lax.broadcasted_iota(jnp.int32, (no, 2 * no), 1)).astype(F32)
    u_re, u_im = prop[0], prop[1]
    u_real = jnp.concatenate(
        [exact(u_re, first) - exact(u_im, second), exact(u_im, first) + exact(u_re, second)], axis=0
    )
    pick = (
        lax.rem(lax.broadcasted_iota(jnp.int32, (2 * no, 128), 0), no)
        == lax.broadcasted_iota(jnp.int32, (2 * no, 128), 1)
    )

    def scaled(d_row):
        wide = jnp.broadcast_to(d_row, (2 * no, 128))
        return jnp.sum(jnp.where(pick, wide, 0.0), axis=1, keepdims=True) * u_real

    def operators(ref):
        even = scaled(ref[0:1, :])
        odd = scaled(ref[1:2, :])
        both = exact(odd, even)
        return even, odd, both

    a_even, a_odd, b_mine = operators(dmine)
    a_odd_s = split(a_odd)
    m_mine = jnp.concatenate([a_even, b_mine], axis=0)
    x0 = jnp.concatenate([l_re[0:no], l_im[0:no]], axis=0)
    start = mm3(split(a_even), split(x0))
    start = jnp.where(me_sa == 0, start, jnp.zeros_like(start))

    for k in range(1, n_sa):
        sa_wait(dall, s_d, r_d, k)
    ops = []
    for q in range(n_sa):
        even, odd, both = operators(dall.at[q])
        ops.append(split(jnp.concatenate([even, both], axis=0)))
    current = jnp.zeros((4 * no, 2 * no), F32)
    for q in range(n_sa - 1, -1, -1):
        if q < n_sa - 1:
            nxt = ops[q + 1]
            current = mm3(split(current), (nxt[0][2 * no :], nxt[1][2 * no :]))
        current = jnp.where(me_sa == q + 1, m_mine, current)
        high, low = split(current)
        w_hi[q] = high
        w_lo[q] = low

    def forced(spec, history):
        acc = None
        for c in range(n_tp):
            part = mm(spec[c], history[c * cols : (c + 1) * cols, :])
            acc = part if acc is None else acc + part
        re = scale * (acc[0:rows, 0:cols] - acc[rows:, cols:])
        im = scale * (acc[0:rows, cols:] + acc[rows:, 0:cols])
        return (
            jnp.concatenate([re[0:no], im[0:no]], axis=0),
            jnp.concatenate([re[no:], im[no:]], axis=0),
        )

    def offsets(f_even, f_odd):
        f_even = f_even + start
        return f_even, mm3(a_odd_s, split(f_even)) + f_odd

    def own_rows(stack, f_even, offset):
        total = jnp.concatenate([f_even, offset], axis=0)
        for q in range(n_sa):
            block = stack[q]
            total = total + (mm(w_hi[q], block) + mm(w_lo[q], block))
        return total

    for k in range(1, n_sa):
        sa_wait(hist, s_h, r_h, k)
    for k in range(1, n_tp):
        tp_wait(spec1, s_s1, r_s1, k)
    f1_even, f1_odd = forced(spec1, hist[...].reshape(n_sa * rows, 2 * cols))
    fe, offset = offsets(f1_even, f1_odd)
    off[me_sa] = offset.astype(BF16)
    fev[me_sa] = fe.astype(BF16)
    send_sa(off, s_o, r_o)
    send_sa(fev, s_f, r_f)
    for k in range(1, n_sa):
        sa_wait(off, s_o, r_o, k)
    mine = own_rows(off, fe, offset)
    p_re = jnp.concatenate([mine[0:no], mine[2 * no : 3 * no]], axis=0)
    p_im = jnp.concatenate([mine[no : 2 * no], mine[3 * no :]], axis=0)
    spec2[me_tp] = spectral_of(p_re, p_im, g_re, g_im, factor)
    send_tp(spec2, s_s2, r_s2)

    for k in range(1, n_sa):
        sa_wait(fev, s_f, r_f, k)
    state = None
    for q in range(n_sa):
        x_even = fev[q].astype(F32)
        x_odd = off[q].astype(F32)
        if state is not None:
            moved = mm3(ops[q], split(state))
            x_even = x_even + moved[0 : 2 * no]
            x_odd = x_odd + moved[2 * no :]
        hist2[q, 0:no, 0:cols] = x_even[0:no].astype(BF16)
        hist2[q, 0:no, cols:] = x_even[no:].astype(BF16)
        hist2[q, no:, 0:cols] = x_odd[0:no].astype(BF16)
        hist2[q, no:, cols:] = x_odd[no:].astype(BF16)
        state = x_odd

    for k in range(1, n_tp):
        tp_wait(spec2, s_s2, r_s2, k)
    f2_even, f2_odd = forced(spec2, hist2[...].reshape(n_sa * rows, 2 * cols))
    fe2, offset2 = offsets(0.5 * (f1_even + f2_even), 0.5 * (f1_odd + f2_odd))
    off2[me_sa] = offset2.astype(BF16)
    send_sa(off2, s_o2, r_o2)
    for k in range(1, n_sa):
        sa_wait(off2, s_o2, r_o2, k)
    final = own_rows(off2, fe2, offset2)
    out[0, 0] = final[0:no]
    out[1, 0] = final[no : 2 * no]
    out[0, 1] = final[2 * no : 3 * no]
    out[1, 1] = final[3 * no :]
    for copy in pending:
        copy.wait_send()


def shards(window, damping, propagator, coupling):
    n_sa, n_tp = lax.axis_size("sa"), lax.axis_size("tp")
    no = coupling.shape[0]
    block = window.shape[2]
    cols = window.shape[4]
    rows = block * no
    scale = 1.0 / (block * n_sa * math.sqrt(no))
    dma = lambda n: pltpu.SemaphoreType.DMA((n,))
    vm = pl.BlockSpec(memory_space=pltpu.VMEM)
    pairs = []
    for n in (n_sa, n_sa, n_tp, n_sa, n_sa, n_tp, n_sa):
        pairs += [dma(n), dma(n)]
    return pl.pallas_call(
        functools.partial(kernel, n_sa, n_tp, scale),
        out_shape=jax.ShapeDtypeStruct((2, block, no, cols), F32),
        in_specs=[vm] * 4,
        out_specs=vm,
        scratch_shapes=[
            pltpu.VMEM((n_sa, 8, 128), F32),
            pltpu.VMEM((n_sa, rows, 2 * cols), BF16),
            pltpu.VMEM((n_tp, 2 * rows, cols), BF16),
            pltpu.VMEM((n_sa, 2 * no, cols), BF16),
            pltpu.VMEM((n_sa, 2 * no, cols), BF16),
            pltpu.VMEM((n_sa, rows, 2 * cols), BF16),
            pltpu.VMEM((n_tp, 2 * rows, cols), BF16),
            pltpu.VMEM((n_sa, 2 * no, cols), BF16),
            pltpu.VMEM((n_sa, 4 * no, 2 * no), BF16),
            pltpu.VMEM((n_sa, 4 * no, 2 * no), BF16),
        ] + pairs,
        compiler_params=pltpu.CompilerParams(collective_id=0, has_side_effects=True),
        name="kadanoff",
    )(window, damping, propagator, coupling.reshape(1, no))


def solution(mesh):
    return jax.shard_map(
        shards,
        mesh=mesh,
        in_specs=(P(None, None, "sa", None, "tp"), P("sa", None), P(), P()),
        out_specs=P(None, "sa", None, "tp"),
        check_vma=False,
    )
```

```python
import functools
import math

import jax
import jax.numpy as jnp
from jax import lax
from jax.experimental import pallas as pl
from jax.experimental.pallas import tpu as pltpu
from jax.sharding import PartitionSpec as P

MESH = pl.DeviceIdType.MESH
F32 = jnp.float32
BF16 = jnp.bfloat16


def exact(a, b):
    return jnp.dot(a, b, precision=lax.Precision.HIGHEST, preferred_element_type=F32)


def split(x):
    high = x.astype(BF16)
    return high, (x - high.astype(F32)).astype(BF16)


def mm(a, b):
    return jnp.dot(a, b, preferred_element_type=F32)


def mm3(a, b):
    return mm(a[0], b[0]) + (mm(a[0], b[1]) + mm(a[1], b[0]))


def spectral_of(x_re, x_im, g_re, g_im, factor):
    lsquare_re = x_re * x_re - x_im * x_im
    lsquare_im = 2.0 * x_re * x_im
    gsquare_re = g_re * g_re - g_im * g_im
    gsquare_im = 2.0 * g_re * g_im
    sless_re = -factor * (lsquare_re * g_re + lsquare_im * g_im)
    sless_im = -factor * (lsquare_im * g_re - lsquare_re * g_im)
    sgreat_re = -factor * (gsquare_re * x_re + gsquare_im * x_im)
    sgreat_im = -factor * (gsquare_im * x_re - gsquare_re * x_im)
    return jnp.concatenate([sgreat_re - sless_re, sgreat_im - sless_im], axis=0).astype(BF16)


def kernel(
    n_sa, n_tp, scale,
    win_in, damp_in, prop_in, coup_in, out,
    win, damp, prop, coup, s_in, dall, hist, spec1, off, fev, hist2, spec2, off2, w_hi, w_lo,
    s_d, r_d, s_h, r_h, s_s1, r_s1, s_o, r_o, s_f, r_f, s_s2, r_s2, s_o2, r_o2,
):
    me_sa = lax.axis_index("sa")
    me_tp = lax.axis_index("tp")
    no = prop.shape[1]
    cols = win.shape[4]
    rows = win.shape[2] * no

    barrier = pltpu.get_barrier_semaphore()
    for k in range(1, n_sa):
        pl.semaphore_signal(
            barrier, inc=1, device_id=(lax.rem(me_sa + k, n_sa), me_tp), device_id_type=MESH
        )
    for k in range(1, n_tp):
        pl.semaphore_signal(
            barrier, inc=1, device_id=(me_sa, lax.rem(me_tp + k, n_tp)), device_id_type=MESH
        )

    loads = [
        pltpu.make_async_copy(src, dst, s_in.at[n])
        for n, (src, dst) in enumerate(
            [(win_in, win), (coup_in, coup), (damp_in, damp), (prop_in, prop)]
        )
    ]
    for load in loads:
        load.start()

    def sa_copy(buf, send, recv, k):
        return pltpu.make_async_remote_copy(
            src_ref=buf.at[me_sa], dst_ref=buf.at[me_sa], send_sem=send.at[k - 1],
            recv_sem=recv.at[me_sa],
            device_id=(lax.rem(me_sa + k, n_sa), me_tp), device_id_type=MESH,
        )

    def sa_wait(buf, send, recv, k):
        who = lax.rem(me_sa + k, n_sa)
        pltpu.make_async_remote_copy(
            src_ref=buf.at[who], dst_ref=buf.at[who], send_sem=send.at[k - 1],
            recv_sem=recv.at[who], device_id=(who, me_tp), device_id_type=MESH,
        ).wait_recv()

    def tp_copy(buf, send, recv, k):
        return pltpu.make_async_remote_copy(
            src_ref=buf.at[me_tp], dst_ref=buf.at[me_tp], send_sem=send.at[k - 1],
            recv_sem=recv.at[me_tp],
            device_id=(me_sa, lax.rem(me_tp + k, n_tp)), device_id_type=MESH,
        )

    def tp_wait(buf, send, recv, k):
        who = lax.rem(me_tp + k, n_tp)
        pltpu.make_async_remote_copy(
            src_ref=buf.at[who], dst_ref=buf.at[who], send_sem=send.at[k - 1],
            recv_sem=recv.at[who], device_id=(me_sa, who), device_id_type=MESH,
        ).wait_recv()

    pending = []

    def send_sa(buf, send, recv):
        for k in range(1, n_sa):
            copy = sa_copy(buf, send, recv, k)
            copy.start()
            pending.append(copy)

    def send_tp(buf, send, recv):
        for k in range(1, n_tp):
            copy = tp_copy(buf, send, recv, k)
            copy.start()
            pending.append(copy)

    for load in loads:
        load.wait()
    row_id = lax.broadcasted_iota(jnp.int32, (no, cols), 0)
    lane_id = lax.broadcasted_iota(jnp.int32, (no, cols), 1)
    tiled = (lax.rem(lane_id, no) == row_id).astype(F32)
    c_row = coup[...]
    c_lanes = exact(c_row, tiled)
    eye = lax.broadcasted_iota(jnp.int32, (no, no), 0) == lax.broadcasted_iota(jnp.int32, (no, no), 1)
    c_col = jnp.sum(jnp.where(eye, jnp.broadcast_to(c_row, (no, no)), 0.0), axis=1, keepdims=True)
    factor = c_col * c_lanes
    factor = jnp.concatenate([factor] * win.shape[2], axis=0)

    l_re = win[0, 0].reshape(rows, cols)
    l_im = win[0, 1].reshape(rows, cols)
    g_re = win[1, 0].reshape(rows, cols)
    g_im = win[1, 1].reshape(rows, cols)
    off2[...] = jnp.zeros(off2.shape, BF16)
    dmine = dall.at[me_sa]
    dmine[...] = jnp.zeros(dmine.shape, F32)
    dmine[0:2, 0:no] = damp[...]
    hmine = hist.at[me_sa]
    hmine[:, 0:cols] = l_re.astype(BF16)
    hmine[:, cols : 2 * cols] = l_im.astype(BF16)
    spec1[me_tp] = spectral_of(l_re, l_im, g_re, g_im, factor)

    first = (lax.broadcasted_iota(jnp.int32, (no, 2 * no), 0)
             == lax.broadcasted_iota(jnp.int32, (no, 2 * no), 1)).astype(F32)
    second = (lax.broadcasted_iota(jnp.int32, (no, 2 * no), 0) + no
              == lax.broadcasted_iota(jnp.int32, (no, 2 * no), 1)).astype(F32)
    u_re, u_im = prop[0], prop[1]
    u_real = jnp.concatenate(
        [exact(u_re, first) - exact(u_im, second), exact(u_im, first) + exact(u_re, second)], axis=0
    )
    pick = (
        lax.rem(lax.broadcasted_iota(jnp.int32, (2 * no, 128), 0), no)
        == lax.broadcasted_iota(jnp.int32, (2 * no, 128), 1)
    )

    def scaled(d_row):
        wide = jnp.broadcast_to(d_row, (2 * no, 128))
        return jnp.sum(jnp.where(pick, wide, 0.0), axis=1, keepdims=True) * u_real

    def operators(ref):
        even = scaled(ref[0:1, :])
        odd = scaled(ref[1:2, :])
        both = exact(odd, even)
        return even, odd, both

    a_even, a_odd, b_mine = operators(dmine)
    a_odd_s = split(a_odd)
    m_mine = jnp.concatenate([a_even, b_mine], axis=0)
    x0 = jnp.concatenate([l_re[0:no], l_im[0:no]], axis=0)
    start = mm3(split(a_even), split(x0))
    start = jnp.where(me_sa == 0, start, jnp.zeros_like(start))

    pl.semaphore_wait(barrier, n_sa + n_tp - 2)
    send_tp(spec1, s_s1, r_s1)
    send_sa(dall, s_d, r_d)
    send_sa(hist, s_h, r_h)

    def forced(spec, history):
        acc = None
        for c in range(n_tp):
            part = mm(spec[c], history[c * cols : (c + 1) * cols, :])
            acc = part if acc is None else acc + part
        re = scale * (acc[0:rows, 0:cols] - acc[rows:, cols:])
        im = scale * (acc[0:rows, cols:] + acc[rows:, 0:cols])
        return (
            jnp.concatenate([re[0:no], im[0:no]], axis=0),
            jnp.concatenate([re[no:], im[no:]], axis=0),
        )

    def offsets(f_even, f_odd):
        f_even = f_even + start
        return f_even, mm3(a_odd_s, split(f_even)) + f_odd

    def own_rows(stack, f_even, offset):
        total = jnp.concatenate([f_even, offset], axis=0)
        for q in range(n_sa):
            block = stack[q]
            total = total + (mm(w_hi[q], block) + mm(w_lo[q], block))
        return total

    for k in range(1, n_sa):
        sa_wait(hist, s_h, r_h, k)
    for k in range(1, n_tp):
        tp_wait(spec1, s_s1, r_s1, k)
    f1_even, f1_odd = forced(spec1, hist[...].reshape(n_sa * rows, 2 * cols))
    fe, offset = offsets(f1_even, f1_odd)
    off[me_sa] = offset.astype(BF16)
    fev[me_sa] = fe.astype(BF16)
    send_sa(off, s_o, r_o)
    send_sa(fev, s_f, r_f)
    for k in range(1, n_sa):
        sa_wait(dall, s_d, r_d, k)
    ops = []
    for q in range(n_sa):
        even, odd, both = operators(dall.at[q])
        ops.append(split(jnp.concatenate([even, both], axis=0)))
    current = jnp.zeros((4 * no, 2 * no), F32)
    for q in range(n_sa - 1, -1, -1):
        if q < n_sa - 1:
            nxt = ops[q + 1]
            current = mm3(split(current), (nxt[0][2 * no :], nxt[1][2 * no :]))
        current = jnp.where(me_sa == q + 1, m_mine, current)
        high, low = split(current)
        w_hi[q] = high
        w_lo[q] = low

    for k in range(1, n_sa):
        sa_wait(off, s_o, r_o, k)
    mine = own_rows(off, fe, offset)
    p_re = jnp.concatenate([mine[0:no], mine[2 * no : 3 * no]], axis=0)
    p_im = jnp.concatenate([mine[no : 2 * no], mine[3 * no :]], axis=0)
    spec2[me_tp] = spectral_of(p_re, p_im, g_re, g_im, factor)
    send_tp(spec2, s_s2, r_s2)

    for k in range(1, n_sa):
        sa_wait(fev, s_f, r_f, k)
    state = None
    for q in range(n_sa):
        x_even = fev[q].astype(F32)
        x_odd = off[q].astype(F32)
        if state is not None:
            moved = mm3(ops[q], split(state))
            x_even = x_even + moved[0 : 2 * no]
            x_odd = x_odd + moved[2 * no :]
        hist2[q, 0:no, 0:cols] = x_even[0:no].astype(BF16)
        hist2[q, 0:no, cols:] = x_even[no:].astype(BF16)
        hist2[q, no:, 0:cols] = x_odd[0:no].astype(BF16)
        hist2[q, no:, cols:] = x_odd[no:].astype(BF16)
        state = x_odd

    for k in range(1, n_tp):
        tp_wait(spec2, s_s2, r_s2, k)
    f2_even, f2_odd = forced(spec2, hist2[...].reshape(n_sa * rows, 2 * cols))
    fe2, offset2 = offsets(0.5 * (f1_even + f2_even), 0.5 * (f1_odd + f2_odd))
    off2[me_sa] = offset2.astype(BF16)
    for k in range(n_sa - 1, 0, -1):

        @pl.when(me_sa + k < n_sa)
        def _():
            sa_copy(off2, s_o2, r_o2, k).start()

    for k in range(1, n_sa):

        @pl.when(me_sa - k >= 0)
        def _():
            sa_wait(off2, s_o2, r_o2, n_sa - k)

    final = own_rows(off2, fe2, offset2)
    out[0, 0] = final[0:no]
    out[1, 0] = final[no : 2 * no]
    out[0, 1] = final[2 * no : 3 * no]
    out[1, 1] = final[3 * no :]
    for k in range(n_sa - 1, 0, -1):

        @pl.when(me_sa + k < n_sa)
        def _():
            sa_copy(off2, s_o2, r_o2, k).wait_send()

    for copy in pending:
        copy.wait_send()


def shards(window, damping, propagator, coupling):
    n_sa, n_tp = lax.axis_size("sa"), lax.axis_size("tp")
    no = coupling.shape[0]
    block = window.shape[2]
    cols = window.shape[4]
    rows = block * no
    scale = 1.0 / (block * n_sa * math.sqrt(no))
    dma = lambda n: pltpu.SemaphoreType.DMA((n,))
    vm = pl.BlockSpec(memory_space=pltpu.VMEM)
    pairs = []
    for n in (n_sa, n_sa, n_tp, n_sa, n_sa, n_tp, n_sa):
        pairs += [dma(n), dma(n)]
    return pl.pallas_call(
        functools.partial(kernel, n_sa, n_tp, scale),
        out_shape=pltpu.VMEM((2, block, no, cols), F32),
        in_specs=[pl.BlockSpec(memory_space=pl.ANY)] * 4,
        out_specs=vm,
        scratch_shapes=[
            pltpu.VMEM(window.shape, F32),
            pltpu.VMEM(damping.shape, F32),
            pltpu.VMEM(propagator.shape, F32),
            pltpu.VMEM((1, no), F32),
            dma(4),
            pltpu.VMEM((n_sa, 8, 128), F32),
            pltpu.VMEM((n_sa, rows, 2 * cols), BF16),
            pltpu.VMEM((n_tp, 2 * rows, cols), BF16),
            pltpu.VMEM((n_sa, 2 * no, cols), BF16),
            pltpu.VMEM((n_sa, 2 * no, cols), BF16),
            pltpu.VMEM((n_sa, rows, 2 * cols), BF16),
            pltpu.VMEM((n_tp, 2 * rows, cols), BF16),
            pltpu.VMEM((n_sa, 2 * no, cols), BF16),
            pltpu.VMEM((n_sa, 4 * no, 2 * no), BF16),
            pltpu.VMEM((n_sa, 4 * no, 2 * no), BF16),
        ] + pairs,
        compiler_params=pltpu.CompilerParams(collective_id=0, has_side_effects=True),
        name="kadanoff",
    )(window, damping, propagator, coupling.reshape(1, no))


def solution(mesh):
    return jax.shard_map(
        shards,
        mesh=mesh,
        in_specs=(P(None, None, "sa", None, "tp"), P("sa", None), P(), P()),
        out_specs=P(None, "sa", None, "tp"),
        check_vma=False,
    )
```

```python
import functools
import math

import jax
import jax.numpy as jnp
from jax import lax
from jax.experimental import pallas as pl
from jax.experimental.pallas import tpu as pltpu
from jax.sharding import PartitionSpec as P

MESH = pl.DeviceIdType.MESH
F32 = jnp.float32
BF16 = jnp.bfloat16


def exact(a, b):
    return jnp.dot(a, b, precision=lax.Precision.HIGHEST, preferred_element_type=F32)


def split(x):
    high = x.astype(BF16)
    return high, (x - high.astype(F32)).astype(BF16)


def mm(a, b):
    return jnp.dot(a, b, preferred_element_type=F32)


def mm3(a, b):
    return mm(a[0], b[0]) + (mm(a[0], b[1]) + mm(a[1], b[0]))


def spectral_of(x_re, x_im, g_re, g_im, factor):
    lsquare_re = x_re * x_re - x_im * x_im
    lsquare_im = 2.0 * x_re * x_im
    gsquare_re = g_re * g_re - g_im * g_im
    gsquare_im = 2.0 * g_re * g_im
    sless_re = -factor * (lsquare_re * g_re + lsquare_im * g_im)
    sless_im = -factor * (lsquare_im * g_re - lsquare_re * g_im)
    sgreat_re = -factor * (gsquare_re * x_re + gsquare_im * x_im)
    sgreat_im = -factor * (gsquare_im * x_re - gsquare_re * x_im)
    return jnp.concatenate([sgreat_re - sless_re, sgreat_im - sless_im], axis=0).astype(BF16)


def kernel(
    n_sa, n_tp, scale,
    win_in, damp_in, prop_in, coup_in, out,
    win, damp, prop, coup, s_in, dall, hist, spec1, off, hist2, spec2, off2, w_hi, w_lo,
    s_d, r_d, s_h, r_h, s_s1, r_s1, s_o, r_o, s_f, r_f, s_s2, r_s2, s_o2, r_o2,
):
    me_sa = lax.axis_index("sa")
    me_tp = lax.axis_index("tp")
    no = prop.shape[1]
    cols = win.shape[4]
    rows = win.shape[2] * no

    barrier = pltpu.get_barrier_semaphore()
    for k in range(1, n_sa):
        pl.semaphore_signal(
            barrier, inc=1, device_id=(lax.rem(me_sa + k, n_sa), me_tp), device_id_type=MESH
        )
    for k in range(1, n_tp):
        pl.semaphore_signal(
            barrier, inc=1, device_id=(me_sa, lax.rem(me_tp + k, n_tp)), device_id_type=MESH
        )

    loads = [
        pltpu.make_async_copy(src, dst, s_in.at[n])
        for n, (src, dst) in enumerate(
            [(win_in, win), (coup_in, coup), (damp_in, damp), (prop_in, prop)]
        )
    ]
    for load in loads:
        load.start()

    def sa_copy(buf, send, recv, k):
        return pltpu.make_async_remote_copy(
            src_ref=buf.at[me_sa], dst_ref=buf.at[me_sa], send_sem=send.at[k - 1],
            recv_sem=recv.at[me_sa],
            device_id=(lax.rem(me_sa + k, n_sa), me_tp), device_id_type=MESH,
        )

    def sa_wait(buf, send, recv, k):
        who = lax.rem(me_sa + k, n_sa)
        pltpu.make_async_remote_copy(
            src_ref=buf.at[who], dst_ref=buf.at[who], send_sem=send.at[k - 1],
            recv_sem=recv.at[who], device_id=(who, me_tp), device_id_type=MESH,
        ).wait_recv()

    def tp_copy(buf, send, recv, k):
        return pltpu.make_async_remote_copy(
            src_ref=buf.at[me_tp], dst_ref=buf.at[me_tp], send_sem=send.at[k - 1],
            recv_sem=recv.at[me_tp],
            device_id=(me_sa, lax.rem(me_tp + k, n_tp)), device_id_type=MESH,
        )

    def tp_wait(buf, send, recv, k):
        who = lax.rem(me_tp + k, n_tp)
        pltpu.make_async_remote_copy(
            src_ref=buf.at[who], dst_ref=buf.at[who], send_sem=send.at[k - 1],
            recv_sem=recv.at[who], device_id=(me_sa, who), device_id_type=MESH,
        ).wait_recv()

    pending = []

    def send_sa(buf, send, recv):
        for k in range(1, n_sa):
            copy = sa_copy(buf, send, recv, k)
            copy.start()
            pending.append(copy)

    def send_tp(buf, send, recv):
        for k in range(1, n_tp):
            copy = tp_copy(buf, send, recv, k)
            copy.start()
            pending.append(copy)

    for load in loads:
        load.wait()
    def send_later(buf, send, recv):
        for k in range(n_sa - 1, 0, -1):

            @pl.when(me_sa + k < n_sa)
            def _():
                sa_copy(buf, send, recv, k).start()

    def drain_later(buf, send, recv):
        for k in range(n_sa - 1, 0, -1):

            @pl.when(me_sa + k < n_sa)
            def _():
                sa_copy(buf, send, recv, k).wait_send()

    def wait_earlier(buf, send, recv):
        for k in range(1, n_sa):

            @pl.when(me_sa - k >= 0)
            def _():
                sa_wait(buf, send, recv, n_sa - k)

    row_id = lax.broadcasted_iota(jnp.int32, (no, cols), 0)
    lane_id = lax.broadcasted_iota(jnp.int32, (no, cols), 1)
    tiled = (lax.rem(lane_id, no) == row_id).astype(F32)
    c_row = coup[...]
    c_lanes = exact(c_row, tiled)
    eye = lax.broadcasted_iota(jnp.int32, (no, no), 0) == lax.broadcasted_iota(jnp.int32, (no, no), 1)
    c_col = jnp.sum(jnp.where(eye, jnp.broadcast_to(c_row, (no, no)), 0.0), axis=1, keepdims=True)
    factor = c_col * c_lanes
    factor = jnp.concatenate([factor] * win.shape[2], axis=0)

    l_re = win[0, 0].reshape(rows, cols)
    l_im = win[0, 1].reshape(rows, cols)
    g_re = win[1, 0].reshape(rows, cols)
    g_im = win[1, 1].reshape(rows, cols)
    off[...] = jnp.zeros(off.shape, BF16)
    off2[...] = jnp.zeros(off2.shape, BF16)
    dmine = dall.at[me_sa]
    dmine[...] = jnp.zeros(dmine.shape, F32)
    dmine[0:2, 0:no] = damp[...]
    hmine = hist.at[me_sa]
    hmine[:, 0:cols] = l_re.astype(BF16)
    hmine[:, cols : 2 * cols] = l_im.astype(BF16)
    spec1[me_tp] = spectral_of(l_re, l_im, g_re, g_im, factor)

    first = (lax.broadcasted_iota(jnp.int32, (no, 2 * no), 0)
             == lax.broadcasted_iota(jnp.int32, (no, 2 * no), 1)).astype(F32)
    second = (lax.broadcasted_iota(jnp.int32, (no, 2 * no), 0) + no
              == lax.broadcasted_iota(jnp.int32, (no, 2 * no), 1)).astype(F32)
    u_re, u_im = prop[0], prop[1]
    u_real = jnp.concatenate(
        [exact(u_re, first) - exact(u_im, second), exact(u_im, first) + exact(u_re, second)], axis=0
    )
    pick = (
        lax.rem(lax.broadcasted_iota(jnp.int32, (2 * no, 128), 0), no)
        == lax.broadcasted_iota(jnp.int32, (2 * no, 128), 1)
    )

    def scaled(d_row):
        wide = jnp.broadcast_to(d_row, (2 * no, 128))
        return jnp.sum(jnp.where(pick, wide, 0.0), axis=1, keepdims=True) * u_real

    def operators(ref):
        even = scaled(ref[0:1, :])
        odd = scaled(ref[1:2, :])
        both = exact(odd, even)
        return even, odd, both

    a_even, a_odd, b_mine = operators(dmine)
    a_odd_s = split(a_odd)
    m_mine = jnp.concatenate([a_even, b_mine], axis=0)
    x0 = jnp.concatenate([l_re[0:no], l_im[0:no]], axis=0)
    start = mm3(split(a_even), split(x0))
    start = jnp.where(me_sa == 0, start, jnp.zeros_like(start))

    pl.semaphore_wait(barrier, n_sa + n_tp - 2)
    send_tp(spec1, s_s1, r_s1)
    send_sa(dall, s_d, r_d)
    send_sa(hist, s_h, r_h)

    def forced(spec, history):
        acc = None
        for c in range(n_tp):
            part = mm(spec[c], history[c * cols : (c + 1) * cols, :])
            acc = part if acc is None else acc + part
        re = scale * (acc[0:rows, 0:cols] - acc[rows:, cols:])
        im = scale * (acc[0:rows, cols:] + acc[rows:, 0:cols])
        return (
            jnp.concatenate([re[0:no], im[0:no]], axis=0),
            jnp.concatenate([re[no:], im[no:]], axis=0),
        )

    def offsets(f_even, f_odd):
        f_even = f_even + start
        return f_even, mm3(a_odd_s, split(f_even)) + f_odd

    def own_rows(stack, f_even, offset):
        total = jnp.concatenate([f_even, offset], axis=0)
        for q in range(n_sa):
            block = stack[q]
            total = total + (mm(w_hi[q], block) + mm(w_lo[q], block))
        return total

    for k in range(1, n_sa):
        sa_wait(hist, s_h, r_h, k)
    for k in range(1, n_tp):
        tp_wait(spec1, s_s1, r_s1, k)
    f1_even, f1_odd = forced(spec1, hist[...].reshape(n_sa * rows, 2 * cols))
    fe, offset = offsets(f1_even, f1_odd)
    off[me_sa] = offset.astype(BF16)
    send_later(off, s_o, r_o)
    for k in range(1, n_sa):
        sa_wait(dall, s_d, r_d, k)
    ops = []
    for q in range(n_sa):
        ops.append(split(operators(dall.at[q])[2]))
    current = jnp.zeros((4 * no, 2 * no), F32)
    for q in range(n_sa - 1, -1, -1):
        if q < n_sa - 1:
            current = mm3(split(current), ops[q + 1])
        current = jnp.where(me_sa == q + 1, m_mine, current)
        high, low = split(current)
        w_hi[q] = high
        w_lo[q] = low

    wait_earlier(off, s_o, r_o)
    mine = own_rows(off, fe, offset)
    p_re = jnp.concatenate([mine[0:no], mine[2 * no : 3 * no]], axis=0)
    p_im = jnp.concatenate([mine[no : 2 * no], mine[3 * no :]], axis=0)
    spec2[me_tp] = spectral_of(p_re, p_im, g_re, g_im, factor)
    send_tp(spec2, s_s2, r_s2)

    h2mine = hist2.at[me_sa]
    h2mine[:, 0:cols] = p_re.astype(BF16)
    h2mine[:, cols:] = p_im.astype(BF16)
    send_sa(hist2, s_f, r_f)
    for k in range(1, n_sa):
        sa_wait(hist2, s_f, r_f, k)
    for k in range(1, n_tp):
        tp_wait(spec2, s_s2, r_s2, k)
    f2_even, f2_odd = forced(spec2, hist2[...].reshape(n_sa * rows, 2 * cols))
    fe2, offset2 = offsets(0.5 * (f1_even + f2_even), 0.5 * (f1_odd + f2_odd))
    off2[me_sa] = offset2.astype(BF16)
    send_later(off2, s_o2, r_o2)
    wait_earlier(off2, s_o2, r_o2)
    final = own_rows(off2, fe2, offset2)
    out[0, 0] = final[0:no]
    out[1, 0] = final[no : 2 * no]
    out[0, 1] = final[2 * no : 3 * no]
    out[1, 1] = final[3 * no :]
    drain_later(off, s_o, r_o)
    drain_later(off2, s_o2, r_o2)
    for copy in pending:
        copy.wait_send()


def shards(window, damping, propagator, coupling):
    n_sa, n_tp = lax.axis_size("sa"), lax.axis_size("tp")
    no = coupling.shape[0]
    block = window.shape[2]
    cols = window.shape[4]
    rows = block * no
    scale = 1.0 / (block * n_sa * math.sqrt(no))
    dma = lambda n: pltpu.SemaphoreType.DMA((n,))
    vm = pl.BlockSpec(memory_space=pltpu.VMEM)
    pairs = []
    for n in (n_sa, n_sa, n_tp, n_sa, n_sa, n_tp, n_sa):
        pairs += [dma(n), dma(n)]
    return pl.pallas_call(
        functools.partial(kernel, n_sa, n_tp, scale),
        out_shape=pltpu.VMEM((2, block, no, cols), F32),
        in_specs=[pl.BlockSpec(memory_space=pl.ANY)] * 4,
        out_specs=vm,
        scratch_shapes=[
            pltpu.VMEM(window.shape, F32),
            pltpu.VMEM(damping.shape, F32),
            pltpu.VMEM(propagator.shape, F32),
            pltpu.VMEM((1, no), F32),
            dma(4),
            pltpu.VMEM((n_sa, 8, 128), F32),
            pltpu.VMEM((n_sa, rows, 2 * cols), BF16),
            pltpu.VMEM((n_tp, 2 * rows, cols), BF16),
            pltpu.VMEM((n_sa, 2 * no, cols), BF16),
            pltpu.VMEM((n_sa, rows, 2 * cols), BF16),
            pltpu.VMEM((n_tp, 2 * rows, cols), BF16),
            pltpu.VMEM((n_sa, 2 * no, cols), BF16),
            pltpu.VMEM((n_sa, 4 * no, 2 * no), BF16),
            pltpu.VMEM((n_sa, 4 * no, 2 * no), BF16),
        ] + pairs,
        compiler_params=pltpu.CompilerParams(collective_id=0, has_side_effects=True),
        name="kadanoff",
    )(window, damping, propagator, coupling.reshape(1, no))


def solution(mesh):
    return jax.shard_map(
        shards,
        mesh=mesh,
        in_specs=(P(None, None, "sa", None, "tp"), P("sa", None), P(), P()),
        out_specs=P(None, "sa", None, "tp"),
        check_vma=False,
    )
```

```python
import functools
import math

import jax
import jax.numpy as jnp
from jax import lax
from jax.experimental import pallas as pl
from jax.experimental.pallas import tpu as pltpu
from jax.sharding import PartitionSpec as P

MESH = pl.DeviceIdType.MESH
F32 = jnp.float32
BF16 = jnp.bfloat16


def exact(a, b):
    return jnp.dot(a, b, precision=lax.Precision.HIGHEST, preferred_element_type=F32)


def split(x):
    high = x.astype(BF16)
    return high, (x - high.astype(F32)).astype(BF16)


def mm(a, b):
    return jnp.dot(a, b, preferred_element_type=F32)


def mm3(a, b):
    return mm(a[0], b[0]) + (mm(a[0], b[1]) + mm(a[1], b[0]))


def spectral_of(x_re, x_im, g_re, g_im, factor):
    lsquare_re = x_re * x_re - x_im * x_im
    lsquare_im = 2.0 * x_re * x_im
    gsquare_re = g_re * g_re - g_im * g_im
    gsquare_im = 2.0 * g_re * g_im
    sless_re = -factor * (lsquare_re * g_re + lsquare_im * g_im)
    sless_im = -factor * (lsquare_im * g_re - lsquare_re * g_im)
    sgreat_re = -factor * (gsquare_re * x_re + gsquare_im * x_im)
    sgreat_im = -factor * (gsquare_im * x_re - gsquare_re * x_im)
    return jnp.concatenate([sgreat_re - sless_re, sgreat_im - sless_im], axis=0).astype(BF16)


def kernel(
    n_sa, n_tp, scale,
    win_in, damp_in, prop_in, coup_in, out,
    win, damp, prop, coup, s_in, dall, hist, spec1, off, back, even2, hist2, spec2, off2, w_hi, w_lo,
    s_d, r_d, s_h, r_h, s_s1, r_s1, s_o, r_o, s_f, r_f, s_s2, r_s2, s_o2, r_o2,
):
    me_sa = lax.axis_index("sa")
    me_tp = lax.axis_index("tp")
    no = prop.shape[1]
    cols = win.shape[4]
    rows = win.shape[2] * no

    barrier = pltpu.get_barrier_semaphore()
    for k in range(1, n_sa):
        pl.semaphore_signal(
            barrier, inc=1, device_id=(lax.rem(me_sa + k, n_sa), me_tp), device_id_type=MESH
        )
    for k in range(1, n_tp):
        pl.semaphore_signal(
            barrier, inc=1, device_id=(me_sa, lax.rem(me_tp + k, n_tp)), device_id_type=MESH
        )

    loads = [
        pltpu.make_async_copy(src, dst, s_in.at[n])
        for n, (src, dst) in enumerate(
            [(win_in, win), (coup_in, coup), (damp_in, damp), (prop_in, prop)]
        )
    ]
    for load in loads:
        load.start()

    def sa_copy(buf, send, recv, k):
        return pltpu.make_async_remote_copy(
            src_ref=buf.at[me_sa], dst_ref=buf.at[me_sa], send_sem=send.at[k - 1],
            recv_sem=recv.at[me_sa],
            device_id=(lax.rem(me_sa + k, n_sa), me_tp), device_id_type=MESH,
        )

    def sa_wait(buf, send, recv, k):
        who = lax.rem(me_sa + k, n_sa)
        pltpu.make_async_remote_copy(
            src_ref=buf.at[who], dst_ref=buf.at[who], send_sem=send.at[k - 1],
            recv_sem=recv.at[who], device_id=(who, me_tp), device_id_type=MESH,
        ).wait_recv()

    def tp_copy(buf, send, recv, k):
        return pltpu.make_async_remote_copy(
            src_ref=buf.at[me_tp], dst_ref=buf.at[me_tp], send_sem=send.at[k - 1],
            recv_sem=recv.at[me_tp],
            device_id=(me_sa, lax.rem(me_tp + k, n_tp)), device_id_type=MESH,
        )

    def tp_wait(buf, send, recv, k):
        who = lax.rem(me_tp + k, n_tp)
        pltpu.make_async_remote_copy(
            src_ref=buf.at[who], dst_ref=buf.at[who], send_sem=send.at[k - 1],
            recv_sem=recv.at[who], device_id=(me_sa, who), device_id_type=MESH,
        ).wait_recv()

    pending = []

    def send_sa(buf, send, recv):
        for k in range(1, n_sa):
            copy = sa_copy(buf, send, recv, k)
            copy.start()
            pending.append(copy)

    def send_tp(buf, send, recv):
        for k in range(1, n_tp):
            copy = tp_copy(buf, send, recv, k)
            copy.start()
            pending.append(copy)

    for load in loads:
        load.wait()
    def back_copy(k):
        return pltpu.make_async_remote_copy(
            src_ref=off.at[me_sa], dst_ref=back.at[me_sa], send_sem=s_o.at[k - 1],
            recv_sem=r_o.at[me_sa],
            device_id=(lax.rem(me_sa + k, n_sa), me_tp), device_id_type=MESH,
        )

    def send_later(buf, send, recv):
        for k in range(n_sa - 1, 0, -1):

            @pl.when(me_sa + k < n_sa)
            def _():
                sa_copy(buf, send, recv, k).start()

    def drain_later(buf, send, recv):
        for k in range(n_sa - 1, 0, -1):

            @pl.when(me_sa + k < n_sa)
            def _():
                sa_copy(buf, send, recv, k).wait_send()

    def wait_earlier(buf, send, recv):
        for k in range(1, n_sa):

            @pl.when(me_sa - k >= 0)
            def _():
                sa_wait(buf, send, recv, n_sa - k)

    row_id = lax.broadcasted_iota(jnp.int32, (no, cols), 0)
    lane_id = lax.broadcasted_iota(jnp.int32, (no, cols), 1)
    tiled = (lax.rem(lane_id, no) == row_id).astype(F32)
    c_row = coup[...]
    c_lanes = exact(c_row, tiled)
    eye = lax.broadcasted_iota(jnp.int32, (no, no), 0) == lax.broadcasted_iota(jnp.int32, (no, no), 1)
    c_col = jnp.sum(jnp.where(eye, jnp.broadcast_to(c_row, (no, no)), 0.0), axis=1, keepdims=True)
    factor = c_col * c_lanes
    factor = jnp.concatenate([factor] * win.shape[2], axis=0)

    l_re = win[0, 0].reshape(rows, cols)
    l_im = win[0, 1].reshape(rows, cols)
    g_re = win[1, 0].reshape(rows, cols)
    g_im = win[1, 1].reshape(rows, cols)
    off[...] = jnp.zeros(off.shape, BF16)
    back[...] = jnp.zeros(back.shape, BF16)
    off2[...] = jnp.zeros(off2.shape, BF16)
    dmine = dall.at[me_sa]
    dmine[...] = jnp.zeros(dmine.shape, F32)
    dmine[0:2, 0:no] = damp[...]
    hmine = hist.at[me_sa]
    hmine[:, 0:cols] = l_re.astype(BF16)
    hmine[:, cols : 2 * cols] = l_im.astype(BF16)
    spec1[me_tp] = spectral_of(l_re, l_im, g_re, g_im, factor)

    first = (lax.broadcasted_iota(jnp.int32, (no, 2 * no), 0)
             == lax.broadcasted_iota(jnp.int32, (no, 2 * no), 1)).astype(F32)
    second = (lax.broadcasted_iota(jnp.int32, (no, 2 * no), 0) + no
              == lax.broadcasted_iota(jnp.int32, (no, 2 * no), 1)).astype(F32)
    u_re, u_im = prop[0], prop[1]
    u_real = jnp.concatenate(
        [exact(u_re, first) - exact(u_im, second), exact(u_im, first) + exact(u_re, second)], axis=0
    )
    pick = (
        lax.rem(lax.broadcasted_iota(jnp.int32, (2 * no, 128), 0), no)
        == lax.broadcasted_iota(jnp.int32, (2 * no, 128), 1)
    )

    def scaled(d_row):
        wide = jnp.broadcast_to(d_row, (2 * no, 128))
        return jnp.sum(jnp.where(pick, wide, 0.0), axis=1, keepdims=True) * u_real

    def operators(ref):
        even = scaled(ref[0:1, :])
        odd = scaled(ref[1:2, :])
        both = exact(odd, even)
        return even, odd, both

    a_even, a_odd, b_mine = operators(dmine)
    a_odd_s = split(a_odd)
    m_mine = jnp.concatenate([a_even, b_mine], axis=0)
    x0 = jnp.concatenate([l_re[0:no], l_im[0:no]], axis=0)
    start = mm3(split(a_even), split(x0))
    start = jnp.where(me_sa == 0, start, jnp.zeros_like(start))

    pl.semaphore_wait(barrier, n_sa + n_tp - 2)
    send_tp(spec1, s_s1, r_s1)
    send_sa(dall, s_d, r_d)
    send_sa(hist, s_h, r_h)

    def forced(spec, history):
        acc = None
        for c in range(n_tp):
            part = mm(spec[c], history[c * cols : (c + 1) * cols, :])
            acc = part if acc is None else acc + part
        re = scale * (acc[0:rows, 0:cols] - acc[rows:, cols:])
        im = scale * (acc[0:rows, cols:] + acc[rows:, 0:cols])
        return (
            jnp.concatenate([re[0:no], im[0:no]], axis=0),
            jnp.concatenate([re[no:], im[no:]], axis=0),
        )

    def offsets(f_even, f_odd):
        f_even = f_even + start
        return f_even, mm3(a_odd_s, split(f_even)) + f_odd

    def own_rows(stack, f_even, offset):
        total = jnp.concatenate([f_even, offset], axis=0)
        for q in range(n_sa):
            block = stack[q]
            total = total + (mm(w_hi[q], block) + mm(w_lo[q], block))
        return total

    for k in range(1, n_sa):
        sa_wait(hist, s_h, r_h, k)
    for k in range(1, n_tp):
        tp_wait(spec1, s_s1, r_s1, k)
    f1_even, f1_odd = forced(spec1, hist[...].reshape(n_sa * rows, 2 * cols))
    fe, offset = offsets(f1_even, f1_odd)
    off[me_sa] = offset.astype(BF16)
    send_later(off, s_o, r_o)
    for k in range(1, n_sa):

        @pl.when(me_sa + k >= n_sa)
        def _():
            back_copy(k).start()

    for k in range(1, n_sa):
        sa_wait(dall, s_d, r_d, k)
    ops = []
    for q in range(n_sa):
        ops.append(split(operators(dall.at[q])[2]))
    current = jnp.zeros((4 * no, 2 * no), F32)
    for q in range(n_sa - 1, -1, -1):
        if q < n_sa - 1:
            current = mm3(split(current), ops[q + 1])
        current = jnp.where(me_sa == q + 1, m_mine, current)
        high, low = split(current)
        w_hi[q] = high
        w_lo[q] = low

    wait_earlier(off, s_o, r_o)
    mine = own_rows(off, fe, offset)
    p_re = jnp.concatenate([mine[0:no], mine[2 * no : 3 * no]], axis=0)
    p_im = jnp.concatenate([mine[no : 2 * no], mine[3 * no :]], axis=0)
    spec2[me_tp] = spectral_of(p_re, p_im, g_re, g_im, factor)
    send_tp(spec2, s_s2, r_s2)

    even2[me_sa, :, 0:cols] = p_re[0:no].astype(BF16)
    even2[me_sa, :, cols:] = p_im[0:no].astype(BF16)
    send_sa(even2, s_f, r_f)
    for k in range(1, n_sa):

        @pl.when(me_sa + k < n_sa)
        def _():
            sa_wait(back, s_o, r_o, k)

    state = None
    for q in range(n_sa):
        block = off[q].astype(F32) + back[q].astype(F32)
        state = block if state is None else mm3(ops[q], split(state)) + block
        hist2[q, no:, 0:cols] = state[0:no].astype(BF16)
        hist2[q, no:, cols:] = state[no:].astype(BF16)
    for k in range(1, n_sa):
        sa_wait(even2, s_f, r_f, k)
    hist2[:, 0:no, :] = even2[...]
    for k in range(1, n_tp):
        tp_wait(spec2, s_s2, r_s2, k)
    f2_even, f2_odd = forced(spec2, hist2[...].reshape(n_sa * rows, 2 * cols))
    fe2, offset2 = offsets(0.5 * (f1_even + f2_even), 0.5 * (f1_odd + f2_odd))
    off2[me_sa] = offset2.astype(BF16)
    send_later(off2, s_o2, r_o2)
    wait_earlier(off2, s_o2, r_o2)
    final = own_rows(off2, fe2, offset2)
    out[0, 0] = final[0:no]
    out[1, 0] = final[no : 2 * no]
    out[0, 1] = final[2 * no : 3 * no]
    out[1, 1] = final[3 * no :]
    drain_later(off, s_o, r_o)
    for k in range(1, n_sa):

        @pl.when(me_sa + k >= n_sa)
        def _():
            back_copy(k).wait_send()

    drain_later(off2, s_o2, r_o2)
    for copy in pending:
        copy.wait_send()


def shards(window, damping, propagator, coupling):
    n_sa, n_tp = lax.axis_size("sa"), lax.axis_size("tp")
    no = coupling.shape[0]
    block = window.shape[2]
    cols = window.shape[4]
    rows = block * no
    scale = 1.0 / (block * n_sa * math.sqrt(no))
    dma = lambda n: pltpu.SemaphoreType.DMA((n,))
    vm = pl.BlockSpec(memory_space=pltpu.VMEM)
    pairs = []
    for n in (n_sa, n_sa, n_tp, n_sa, n_sa, n_tp, n_sa):
        pairs += [dma(n), dma(n)]
    return pl.pallas_call(
        functools.partial(kernel, n_sa, n_tp, scale),
        out_shape=pltpu.VMEM((2, block, no, cols), F32),
        in_specs=[pl.BlockSpec(memory_space=pl.ANY)] * 4,
        out_specs=vm,
        scratch_shapes=[
            pltpu.VMEM(window.shape, F32),
            pltpu.VMEM(damping.shape, F32),
            pltpu.VMEM(propagator.shape, F32),
            pltpu.VMEM((1, no), F32),
            dma(4),
            pltpu.VMEM((n_sa, 8, 128), F32),
            pltpu.VMEM((n_sa, rows, 2 * cols), BF16),
            pltpu.VMEM((n_tp, 2 * rows, cols), BF16),
            pltpu.VMEM((n_sa, 2 * no, cols), BF16),
            pltpu.VMEM((n_sa, 2 * no, cols), BF16),
            pltpu.VMEM((n_sa, no, 2 * cols), BF16),
            pltpu.VMEM((n_sa, rows, 2 * cols), BF16),
            pltpu.VMEM((n_tp, 2 * rows, cols), BF16),
            pltpu.VMEM((n_sa, 2 * no, cols), BF16),
            pltpu.VMEM((n_sa, 4 * no, 2 * no), BF16),
            pltpu.VMEM((n_sa, 4 * no, 2 * no), BF16),
        ] + pairs,
        compiler_params=pltpu.CompilerParams(collective_id=0, has_side_effects=True),
        name="kadanoff",
    )(window, damping, propagator, coupling.reshape(1, no))


def solution(mesh):
    return jax.shard_map(
        shards,
        mesh=mesh,
        in_specs=(P(None, None, "sa", None, "tp"), P("sa", None), P(), P()),
        out_specs=P(None, "sa", None, "tp"),
        check_vma=False,
    )
```

```python
import functools
import math

import jax
import jax.numpy as jnp
from jax import lax
from jax.experimental import pallas as pl
from jax.experimental.pallas import tpu as pltpu
from jax.sharding import PartitionSpec as P

MESH = pl.DeviceIdType.MESH
F32 = jnp.float32
BF16 = jnp.bfloat16


def exact(a, b):
    return jnp.dot(a, b, precision=lax.Precision.HIGHEST, preferred_element_type=F32)


def split(x):
    high = x.astype(BF16)
    return high, (x - high.astype(F32)).astype(BF16)


def mm(a, b):
    return jnp.dot(a, b, preferred_element_type=F32)


def mm3(a, b):
    return mm(a[0], b[0]) + (mm(a[0], b[1]) + mm(a[1], b[0]))


def spectral_of(x_re, x_im, g_re, g_im, factor):
    lsquare_re = x_re * x_re - x_im * x_im
    lsquare_im = 2.0 * x_re * x_im
    gsquare_re = g_re * g_re - g_im * g_im
    gsquare_im = 2.0 * g_re * g_im
    sless_re = -factor * (lsquare_re * g_re + lsquare_im * g_im)
    sless_im = -factor * (lsquare_im * g_re - lsquare_re * g_im)
    sgreat_re = -factor * (gsquare_re * x_re + gsquare_im * x_im)
    sgreat_im = -factor * (gsquare_im * x_re - gsquare_re * x_im)
    return jnp.concatenate([sgreat_re - sless_re, sgreat_im - sless_im], axis=0).astype(BF16)


def kernel(
    n_sa, n_tp, scale,
    win_in, damp_in, prop_in, coup_in, out,
    win, damp, prop, coup, s_in, dall, hist, spec1, off, back, even2, hist2, spec2, off2, w_hi, w_lo,
    s_d, r_d, s_h, r_h, s_s1, r_s1, s_o, r_o, s_f, r_f, s_s2, r_s2, s_o2, r_o2,
):
    me_sa = lax.axis_index("sa")
    me_tp = lax.axis_index("tp")
    no = prop.shape[1]
    cols = win.shape[4]
    rows = win.shape[2] * no

    barrier = pltpu.get_barrier_semaphore()
    for k in range(1, n_sa):
        pl.semaphore_signal(
            barrier, inc=1, device_id=(lax.rem(me_sa + k, n_sa), me_tp), device_id_type=MESH
        )
    for k in range(1, n_tp):
        pl.semaphore_signal(
            barrier, inc=1, device_id=(me_sa, lax.rem(me_tp + k, n_tp)), device_id_type=MESH
        )

    loads = [
        pltpu.make_async_copy(src, dst, s_in.at[n])
        for n, (src, dst) in enumerate(
            [(win_in, win), (coup_in, coup), (damp_in, damp), (prop_in, prop)]
        )
    ]
    for load in loads:
        load.start()

    def sa_copy(buf, send, recv, k):
        return pltpu.make_async_remote_copy(
            src_ref=buf.at[me_sa], dst_ref=buf.at[me_sa], send_sem=send.at[k - 1],
            recv_sem=recv.at[me_sa],
            device_id=(lax.rem(me_sa + k, n_sa), me_tp), device_id_type=MESH,
        )

    def sa_wait(buf, send, recv, k):
        who = lax.rem(me_sa + k, n_sa)
        pltpu.make_async_remote_copy(
            src_ref=buf.at[who], dst_ref=buf.at[who], send_sem=send.at[k - 1],
            recv_sem=recv.at[who], device_id=(who, me_tp), device_id_type=MESH,
        ).wait_recv()

    def tp_copy(buf, send, recv, k):
        return pltpu.make_async_remote_copy(
            src_ref=buf.at[me_tp], dst_ref=buf.at[me_tp], send_sem=send.at[k - 1],
            recv_sem=recv.at[me_tp],
            device_id=(me_sa, lax.rem(me_tp + k, n_tp)), device_id_type=MESH,
        )

    def tp_wait(buf, send, recv, k):
        who = lax.rem(me_tp + k, n_tp)
        pltpu.make_async_remote_copy(
            src_ref=buf.at[who], dst_ref=buf.at[who], send_sem=send.at[k - 1],
            recv_sem=recv.at[who], device_id=(me_sa, who), device_id_type=MESH,
        ).wait_recv()

    pending = []

    def send_sa(buf, send, recv):
        for k in range(1, n_sa):
            copy = sa_copy(buf, send, recv, k)
            copy.start()
            pending.append(copy)

    def send_tp(buf, send, recv):
        for k in range(1, n_tp):
            copy = tp_copy(buf, send, recv, k)
            copy.start()
            pending.append(copy)

    for load in loads:
        load.wait()
    def back_copy(k):
        return pltpu.make_async_remote_copy(
            src_ref=off.at[me_sa], dst_ref=back.at[me_sa], send_sem=s_o.at[k - 1],
            recv_sem=r_o.at[me_sa],
            device_id=(lax.rem(me_sa + k, n_sa), me_tp), device_id_type=MESH,
        )

    def send_later(buf, send, recv):
        for k in range(n_sa - 1, 0, -1):

            @pl.when(me_sa + k < n_sa)
            def _():
                sa_copy(buf, send, recv, k).start()

    def drain_later(buf, send, recv):
        for k in range(n_sa - 1, 0, -1):

            @pl.when(me_sa + k < n_sa)
            def _():
                sa_copy(buf, send, recv, k).wait_send()

    def wait_earlier(buf, send, recv):
        for k in range(1, n_sa):

            @pl.when(me_sa - k >= 0)
            def _():
                sa_wait(buf, send, recv, n_sa - k)

    row_id = lax.broadcasted_iota(jnp.int32, (no, cols), 0)
    lane_id = lax.broadcasted_iota(jnp.int32, (no, cols), 1)
    tiled = (lax.rem(lane_id, no) == row_id).astype(F32)
    c_row = coup[...]
    c_lanes = exact(c_row, tiled)
    eye = lax.broadcasted_iota(jnp.int32, (no, no), 0) == lax.broadcasted_iota(jnp.int32, (no, no), 1)
    c_col = jnp.sum(jnp.where(eye, jnp.broadcast_to(c_row, (no, no)), 0.0), axis=1, keepdims=True)
    factor = c_col * c_lanes
    factor = jnp.concatenate([factor] * win.shape[2], axis=0)

    l_re = win[0, 0].reshape(rows, cols)
    l_im = win[0, 1].reshape(rows, cols)
    g_re = win[1, 0].reshape(rows, cols)
    g_im = win[1, 1].reshape(rows, cols)
    off[...] = jnp.zeros(off.shape, BF16)
    back[...] = jnp.zeros(back.shape, BF16)
    off2[...] = jnp.zeros(off2.shape, BF16)
    dmine = dall.at[me_sa]
    dmine[...] = jnp.zeros(dmine.shape, F32)
    dmine[0:2, 0:no] = damp[...]
    hmine = hist.at[me_sa]
    hmine[:, 0:cols] = l_re.astype(BF16)
    hmine[:, cols : 2 * cols] = l_im.astype(BF16)
    spec1[me_tp] = spectral_of(l_re, l_im, g_re, g_im, factor)

    first = (lax.broadcasted_iota(jnp.int32, (no, 2 * no), 0)
             == lax.broadcasted_iota(jnp.int32, (no, 2 * no), 1)).astype(F32)
    second = (lax.broadcasted_iota(jnp.int32, (no, 2 * no), 0) + no
              == lax.broadcasted_iota(jnp.int32, (no, 2 * no), 1)).astype(F32)
    u_re, u_im = prop[0], prop[1]
    u_real = jnp.concatenate(
        [exact(u_re, first) - exact(u_im, second), exact(u_im, first) + exact(u_re, second)], axis=0
    )
    pick = (
        lax.rem(lax.broadcasted_iota(jnp.int32, (2 * no, 128), 0), no)
        == lax.broadcasted_iota(jnp.int32, (2 * no, 128), 1)
    )

    def scaled(d_row):
        wide = jnp.broadcast_to(d_row, (2 * no, 128))
        return jnp.sum(jnp.where(pick, wide, 0.0), axis=1, keepdims=True) * u_real

    def operators(ref):
        even = scaled(ref[0:1, :])
        odd = scaled(ref[1:2, :])
        both = exact(odd, even)
        return even, odd, both

    a_even, a_odd, b_mine = operators(dmine)
    a_odd_s = split(a_odd)
    m_mine = jnp.concatenate([a_even, b_mine], axis=0)
    x0 = jnp.concatenate([l_re[0:no], l_im[0:no]], axis=0)
    start = mm3(split(a_even), split(x0))
    start = jnp.where(me_sa == 0, start, jnp.zeros_like(start))

    pl.semaphore_wait(barrier, n_sa + n_tp - 2)
    send_tp(spec1, s_s1, r_s1)
    send_sa(dall, s_d, r_d)
    send_sa(hist, s_h, r_h)

    def forced(spec, history):
        acc = None
        for c in range(n_tp):
            part = mm(spec[c], history[c * cols : (c + 1) * cols, :])
            acc = part if acc is None else acc + part
        re = scale * (acc[0:rows, 0:cols] - acc[rows:, cols:])
        im = scale * (acc[0:rows, cols:] + acc[rows:, 0:cols])
        return (
            jnp.concatenate([re[0:no], im[0:no]], axis=0),
            jnp.concatenate([re[no:], im[no:]], axis=0),
        )

    def offsets(f_even, f_odd):
        f_even = f_even + start
        return f_even, mm3(a_odd_s, split(f_even)) + f_odd

    def own_rows(stack, f_even, offset):
        total = jnp.concatenate([f_even, offset], axis=0)
        flat = stack[...].reshape(n_sa * 2 * no, cols)
        return total + (mm(w_hi[...], flat) + mm(w_lo[...], flat))

    for k in range(1, n_sa):
        sa_wait(hist, s_h, r_h, k)
    for k in range(1, n_tp):
        tp_wait(spec1, s_s1, r_s1, k)
    f1_even, f1_odd = forced(spec1, hist[...].reshape(n_sa * rows, 2 * cols))
    fe, offset = offsets(f1_even, f1_odd)
    off[me_sa] = offset.astype(BF16)
    send_later(off, s_o, r_o)
    for k in range(1, n_sa):

        @pl.when(me_sa + k >= n_sa)
        def _():
            back_copy(k).start()

    for k in range(1, n_sa):
        sa_wait(dall, s_d, r_d, k)
    ops = []
    for q in range(n_sa):
        ops.append(split(operators(dall.at[q])[2]))
    current = jnp.zeros((4 * no, 2 * no), F32)
    for q in range(n_sa - 1, -1, -1):
        if q < n_sa - 1:
            current = mm3(split(current), ops[q + 1])
        current = jnp.where(me_sa == q + 1, m_mine, current)
        high, low = split(current)
        w_hi[:, 2 * no * q : 2 * no * (q + 1)] = high
        w_lo[:, 2 * no * q : 2 * no * (q + 1)] = low

    wait_earlier(off, s_o, r_o)
    mine = own_rows(off, fe, offset)
    p_re = jnp.concatenate([mine[0:no], mine[2 * no : 3 * no]], axis=0)
    p_im = jnp.concatenate([mine[no : 2 * no], mine[3 * no :]], axis=0)
    spec2[me_tp] = spectral_of(p_re, p_im, g_re, g_im, factor)
    send_tp(spec2, s_s2, r_s2)

    even2[me_sa, :, 0:cols] = p_re[0:no].astype(BF16)
    even2[me_sa, :, cols:] = p_im[0:no].astype(BF16)
    send_sa(even2, s_f, r_f)
    for k in range(1, n_sa):

        @pl.when(me_sa + k < n_sa)
        def _():
            sa_wait(back, s_o, r_o, k)

    state = None
    for q in range(n_sa):
        block = off[q].astype(F32) + back[q].astype(F32)
        state = block if state is None else mm3(ops[q], split(state)) + block
        hist2[q, no:, 0:cols] = state[0:no].astype(BF16)
        hist2[q, no:, cols:] = state[no:].astype(BF16)
    for k in range(1, n_sa):
        sa_wait(even2, s_f, r_f, k)
    hist2[:, 0:no, :] = even2[...]
    for k in range(1, n_tp):
        tp_wait(spec2, s_s2, r_s2, k)
    f2_even, f2_odd = forced(spec2, hist2[...].reshape(n_sa * rows, 2 * cols))
    fe2, offset2 = offsets(0.5 * (f1_even + f2_even), 0.5 * (f1_odd + f2_odd))
    off2[me_sa] = offset2.astype(BF16)
    send_later(off2, s_o2, r_o2)
    wait_earlier(off2, s_o2, r_o2)
    final = own_rows(off2, fe2, offset2)
    out[0, 0] = final[0:no]
    out[1, 0] = final[no : 2 * no]
    out[0, 1] = final[2 * no : 3 * no]
    out[1, 1] = final[3 * no :]
    drain_later(off, s_o, r_o)
    for k in range(1, n_sa):

        @pl.when(me_sa + k >= n_sa)
        def _():
            back_copy(k).wait_send()

    drain_later(off2, s_o2, r_o2)
    for copy in pending:
        copy.wait_send()


def shards(window, damping, propagator, coupling):
    n_sa, n_tp = lax.axis_size("sa"), lax.axis_size("tp")
    no = coupling.shape[0]
    block = window.shape[2]
    cols = window.shape[4]
    rows = block * no
    scale = 1.0 / (block * n_sa * math.sqrt(no))
    dma = lambda n: pltpu.SemaphoreType.DMA((n,))
    vm = pl.BlockSpec(memory_space=pltpu.VMEM)
    pairs = []
    for n in (n_sa, n_sa, n_tp, n_sa, n_sa, n_tp, n_sa):
        pairs += [dma(n), dma(n)]
    return pl.pallas_call(
        functools.partial(kernel, n_sa, n_tp, scale),
        out_shape=pltpu.VMEM((2, block, no, cols), F32),
        in_specs=[pl.BlockSpec(memory_space=pl.ANY)] * 4,
        out_specs=vm,
        scratch_shapes=[
            pltpu.VMEM(window.shape, F32),
            pltpu.VMEM(damping.shape, F32),
            pltpu.VMEM(propagator.shape, F32),
            pltpu.VMEM((1, no), F32),
            dma(4),
            pltpu.VMEM((n_sa, 8, 128), F32),
            pltpu.VMEM((n_sa, rows, 2 * cols), BF16),
            pltpu.VMEM((n_tp, 2 * rows, cols), BF16),
            pltpu.VMEM((n_sa, 2 * no, cols), BF16),
            pltpu.VMEM((n_sa, 2 * no, cols), BF16),
            pltpu.VMEM((n_sa, no, 2 * cols), BF16),
            pltpu.VMEM((n_sa, rows, 2 * cols), BF16),
            pltpu.VMEM((n_tp, 2 * rows, cols), BF16),
            pltpu.VMEM((n_sa, 2 * no, cols), BF16),
            pltpu.VMEM((4 * no, n_sa * 2 * no), BF16),
            pltpu.VMEM((4 * no, n_sa * 2 * no), BF16),
        ] + pairs,
        compiler_params=pltpu.CompilerParams(collective_id=0, has_side_effects=True),
        name="kadanoff",
    )(window, damping, propagator, coupling.reshape(1, no))


def solution(mesh):
    return jax.shard_map(
        shards,
        mesh=mesh,
        in_specs=(P(None, None, "sa", None, "tp"), P("sa", None), P(), P()),
        out_specs=P(None, "sa", None, "tp"),
        check_vma=False,
    )
```
